32 devices in a mesh: chain: 4 (over x, core), col: 8 (over z, y).
Axes of the slice: x: 2, y: 2, z: 4, core: 2. Of those that a mesh axis runs over, the one named last changes fastest.
Arguments:
- rhs: float32 [4, 8, 64, 128], P('chain', 'col'), may hold values from -6 to 6
- inverse: float32 [4, 8, 128, 128], P('chain', 'col'), as said below
- factor: float32 [4, 8, 8, 128, 128], P('chain', 'col'), may hold values from -0.1875 to 0.1875
- pattern: int32 [4, 8, 8], P('chain', 'col'), may hold values from 0 to 7, as said below
Outputs:
- forward: float32 [4, 8, 64, 128], P('chain', 'col')
- solution: float32 [4, 8, 64, 128], P('chain', 'col')
The draws below stay inside these ranges and needn't reach their ends.
Inputs may be any that keep to these rules, and one draw needn't show every extreme that they name: `pattern`: the 8 block rows of one supernode are distinct. `inverse`: each block is lower triangular, its diagonal between 0.5 and 1.5.
All inputs are finite; a program needn't handle non-finite values.
Results may differ from the reference program's by a relative error of at most 0.00012.
Values sent between devices are 32-bit elements; how exact they have to be, the bound alone decides.
A program may use at most 64 MiB of HBM per device.

```python
import jax
import jax.numpy as jnp
from jax import lax

BLOCK = 128
NB = 8
LOADS = 64
LEVELS = 4
SUPS = 8


def draw_inverse(key, part):
    keyed = jax.random.fold_in(key, 7)
    first, second = jax.random.split(keyed)
    diagonal = jax.random.uniform(first, (LEVELS, SUPS, BLOCK), jnp.float32, 0.5, 1.5)
    lower = jax.random.normal(second, (LEVELS, SUPS, BLOCK, BLOCK), jnp.float32) * (0.6 / BLOCK ** 0.5)
    strict = jnp.tril(jnp.ones((BLOCK, BLOCK), jnp.float32), -1)
    return lower * strict + diagonal[..., None] * jnp.eye(BLOCK, dtype=jnp.float32)


def draw_pattern(key, part):
    keyed = jax.random.fold_in(key, 11)
    keys = jax.random.split(keyed, LEVELS * SUPS)
    chosen = jax.vmap(lambda single: jax.random.permutation(single, SUPS)[:NB])(keys)
    return chosen.reshape(LEVELS, SUPS, NB).astype(jnp.int32)


def block_levels(own_key, extent, cuts, smallest, high):
    gain = 1.0
    for axis_at, shards_of in cuts:
        draws = jax.random.uniform(jax.random.fold_in(jax.random.fold_in(own_key, 6), axis_at), (shards_of,), jnp.float32, smallest / len(cuts), high / len(cuts))
        gain = gain * jnp.repeat(jnp.exp(draws), extent[axis_at] // shards_of).reshape((-1,) + (1,) * (len(extent) - 1 - axis_at))
    return gain


def bell_draw(key, dims, scale, limit, shards=(), kind=jnp.bfloat16):
    loudness = block_levels(key, dims, shards, -0.22, 0.18) if shards else 1.0
    values = jax.random.normal(key, dims, jnp.float32) * scale * loudness
    return jnp.minimum(jnp.maximum(values, -limit), limit).astype(kind)


def setup_inputs(seed: int = 0) -> dict:
    key_list = jax.random.split(jax.random.key(seed), 5)
    return {
        "rhs": bell_draw(key_list[0], (LEVELS, SUPS, LOADS, BLOCK), 1.0, 6.0, ((0, 4), (1, 8)), jnp.float32),
        "inverse": draw_inverse(jax.random.fold_in(key_list[4], 71), 0),
        "factor": bell_draw(key_list[2], (LEVELS, SUPS, NB, BLOCK, BLOCK), (BLOCK * NB) ** -0.5, 0.1875, ((0, 4), (1, 8)), jnp.float32),
        "pattern": draw_pattern(jax.random.fold_in(key_list[4], 71), 0),
    }


def reference(rhs, inverse, factor, pattern):
    highest = lax.Precision.HIGHEST
    onehot = (pattern[..., None] == jnp.arange(SUPS, dtype=jnp.int32)).astype(jnp.float32)
    incoming = jnp.zeros((SUPS, LOADS, BLOCK), jnp.float32)
    forward_list = []
    for level in range(LEVELS):
        solved = jnp.einsum("jrb,jab->jra", rhs[level] - incoming, inverse[level], precision=highest)
        forward_list.append(solved)
        terms = jnp.einsum("jrb,jkab->jkra", solved, factor[level], precision=highest)
        incoming = jnp.einsum("jkc,jkra->cra", onehot[level], terms, precision=highest)
    outgoing = jnp.zeros((SUPS, LOADS, BLOCK), jnp.float32)
    solution_list = [None] * LEVELS
    for level in reversed(range(LEVELS)):
        solved = jnp.einsum("jra,jab->jrb", forward_list[level] - outgoing, inverse[level], precision=highest)
        solution_list[level] = solved
        if level > 0:
            picked = jnp.einsum("jkc,cra->jkra", onehot[level - 1], solved, precision=highest)
            outgoing = jnp.einsum("jkra,jkab->jrb", picked, factor[level - 1], precision=highest)
    return jnp.stack(forward_list), jnp.stack(solution_list)
```

```python
import functools

import jax
import jax.numpy as jnp
from jax import lax
from jax.experimental import pallas as pl
from jax.experimental.pallas import tpu as pltpu
from jax.sharding import PartitionSpec as P

PIECES = 2
MESH = pl.DeviceIdType.MESH


def halves(value):
    high = value.astype(jnp.bfloat16)
    low = (value - high.astype(jnp.float32)).astype(jnp.bfloat16)
    return high, low


def times_transposed(value, packed):
    rows = value.shape[0]
    high, low = halves(value)
    stacked = jnp.concatenate(
        [jnp.concatenate([high, low], axis=1), jnp.concatenate([low, high], axis=1)], axis=0
    )
    both = lax.dot_general(
        stacked, packed, (((1,), (1,)), ((), ())), preferred_element_type=jnp.float32
    )
    return both[:rows] + both[rows:]


def times(value, packed):
    rows = value.shape[0]
    width = packed.shape[1] // 2
    high, low = halves(value)
    both = jnp.dot(
        jnp.concatenate([high, low], axis=0), packed, preferred_element_type=jnp.float32
    )
    summed = both[:rows] + both[rows:]
    return summed[:, :width] + summed[:, width:]


def kernel(
    levels, supers, rhs_hbm, inverse_hbm, factor_hbm, pattern_hbm, forward_ref, answer_ref,
    rhs, inverse, factor, pattern, inverse_packed, factor_packed, terms, outbox, inbox, solved,
    load_sem, outbox_sem, inbox_sem, solved_sem, arrived_sem, *arrived,
):
    place = lax.axis_index("chain")
    me = lax.axis_index("col")
    count, _, width = factor.shape
    loads = rhs.shape[0]
    rows = loads // PIECES
    loading = [
        pltpu.make_async_copy(source, target, load_sem.at[at])
        for at, (source, target) in enumerate(
            ((rhs_hbm, rhs), (inverse_hbm, inverse), (factor_hbm, factor), (pattern_hbm, pattern))
        )
    ]
    for copy in loading:
        copy.start()
    peers = [lax.rem(me + shift, supers) for shift in range(supers)]

    barrier = pltpu.get_barrier_semaphore()

    @pl.when(place > 0)
    def _():
        for peer in peers:
            pl.semaphore_signal(
                barrier, inc=1, device_id={"chain": place - 1, "col": peer}, device_id_type=MESH
            )

    @pl.when(place < levels - 1)
    def _():
        for peer in peers:
            pl.semaphore_signal(
                barrier, inc=1, device_id={"chain": place + 1, "col": peer}, device_id_type=MESH
            )

    loading[0].wait()
    loading[1].wait()
    high, low = halves(inverse[...])
    inverse_packed[:, :width] = high
    inverse_packed[:, width:] = low
    loading[2].wait()
    for block in range(count):
        high, low = halves(factor[block])
        factor_packed[block * width:(block + 1) * width, :width] = high
        factor_packed[block * width:(block + 1) * width, width:] = low
    loading[3].wait()
    targets = [pattern[0, 0, block] for block in range(count)]
    origin = []
    for peer in peers:
        at = jnp.int32(-1)
        for block in range(count):
            at = jnp.where(targets[block] == peer, jnp.int32(block), at)
        origin.append(at)
    slots = [lax.rem(me - target + supers, supers) for target in targets]

    pl.semaphore_wait(
        barrier, jnp.where(place > 0, supers, 0) + jnp.where(place < levels - 1, supers, 0)
    )

    def term_copy(piece, shift):
        return pltpu.make_async_remote_copy(
            src_ref=outbox.at[piece, shift],
            dst_ref=inbox.at[piece, shift],
            send_sem=outbox_sem.at[piece, shift],
            recv_sem=inbox_sem.at[piece, shift],
            device_id={"chain": place + 1, "col": peers[shift]},
            device_id_type=MESH,
        )

    def answer_copy(piece, shift):
        return pltpu.make_async_remote_copy(
            src_ref=solved.at[piece],
            dst_ref=arrived[piece].at[shift],
            send_sem=solved_sem.at[piece, shift],
            recv_sem=arrived_sem.at[piece, shift],
            device_id={"chain": place - 1, "col": peers[shift]},
            device_id_type=MESH,
        )

    for piece in range(PIECES):
        part = pl.ds(piece * rows, rows)

        @pl.when(place > 0)
        def _():
            total = rhs[part, :]
            for shift in range(supers):
                pltpu.make_async_copy(
                    inbox.at[piece, shift], inbox.at[piece, shift], inbox_sem.at[piece, shift]
                ).wait()
                total = total - inbox[piece, shift]
            rhs[part, :] = total

        fresh = times_transposed(rhs[part, :], inverse_packed[...])
        forward_ref[part, :] = fresh

        @pl.when(place < levels - 1)
        def _():
            wide = times_transposed(fresh, factor_packed[...])
            for block in range(count):
                terms[block] = wide[:, block * width:(block + 1) * width]
            for shift in range(supers):
                picked = terms[jnp.maximum(origin[shift], 0)]
                if count < supers:
                    picked = jnp.where(origin[shift] >= 0, picked, 0.0)
                outbox[piece, shift] = picked
                term_copy(piece, shift).start()

    for piece in range(PIECES):
        part = pl.ds(piece * rows, rows)
        rhs[part, :] = forward_ref[part, :]

        @pl.when(place < levels - 1)
        def _():
            for shift in range(supers):
                pltpu.make_async_copy(
                    arrived[piece].at[shift], arrived[piece].at[shift], arrived_sem.at[piece, shift]
                ).wait()
            picked = jnp.concatenate([arrived[piece][slot] for slot in slots], axis=1)
            rhs[part, :] = rhs[part, :] - times(picked, factor_packed[...])

        fresh = times(rhs[part, :], inverse_packed[...])
        solved[piece] = fresh
        answer_ref[part, :] = fresh

        @pl.when(place > 0)
        def _():
            for shift in range(supers):
                answer_copy(piece, shift).start()

    @pl.when(place < levels - 1)
    def _():
        for piece in range(PIECES):
            for shift in range(supers):
                term_copy(piece, shift).wait_send()

    @pl.when(place > 0)
    def _():
        for piece in range(PIECES):
            for shift in range(supers):
                answer_copy(piece, shift).wait_send()


def body(rhs, inverse, factor, pattern):
    levels = lax.axis_size("chain")
    supers = lax.axis_size("col")
    loads, width = rhs.shape[2:]
    count = factor.shape[2]
    rows = loads // PIECES
    block = jax.ShapeDtypeStruct((loads, width), jnp.float32)
    anywhere = pl.BlockSpec(memory_space=pl.ANY)
    solved, answer = pl.pallas_call(
        functools.partial(kernel, levels, supers),
        out_shape=(block, block),
        in_specs=[anywhere] * 4,
        out_specs=[pl.BlockSpec(memory_space=pltpu.VMEM)] * 2,
        scratch_shapes=[
            pltpu.VMEM((loads, width), jnp.float32),
            pltpu.VMEM((width, width), jnp.float32),
            pltpu.VMEM((count, width, width), jnp.float32),
            pltpu.SMEM((1, 1, count), jnp.int32),
            pltpu.VMEM((width, 2 * width), jnp.bfloat16),
            pltpu.VMEM((count * width, 2 * width), jnp.bfloat16),
            pltpu.VMEM((count, rows, width), jnp.float32),
            pltpu.VMEM((PIECES, supers, rows, width), jnp.float32),
            pltpu.VMEM((PIECES, supers, rows, width), jnp.float32),
            pltpu.VMEM((PIECES, rows, width), jnp.float32),
            pltpu.SemaphoreType.DMA((4,)),
            pltpu.SemaphoreType.DMA((PIECES, supers)),
            pltpu.SemaphoreType.DMA((PIECES, supers)),
            pltpu.SemaphoreType.DMA((PIECES, supers)),
            pltpu.SemaphoreType.DMA((PIECES, supers)),
            *[pltpu.VMEM((supers, rows, width), jnp.float32)] * PIECES,
        ],
        compiler_params=pltpu.CompilerParams(collective_id=0, has_side_effects=True),
    )(rhs[0, 0], inverse[0, 0], factor[0, 0], pattern)
    return (solved[None, None], answer[None, None])


def solution(mesh):
    in_specs = (
        P("chain", "col", None, None),
        P("chain", "col", None, None),
        P("chain", "col", None, None, None),
        P("chain", "col", None),
    )
    out_specs = (P("chain", "col", None, None), P("chain", "col", None, None))
    return jax.shard_map(body, mesh=mesh, in_specs=in_specs, out_specs=out_specs, check_vma=False)
```

```python
import functools

import jax
import jax.numpy as jnp
from jax import lax
from jax.experimental import pallas as pl
from jax.experimental.pallas import tpu as pltpu
from jax.sharding import PartitionSpec as P

PIECES = 4
MESH = pl.DeviceIdType.MESH


def halves(value):
    high = value.astype(jnp.bfloat16)
    low = (value - high.astype(jnp.float32)).astype(jnp.bfloat16)
    return high, low


def times_transposed(value, packed):
    rows = value.shape[0]
    high, low = halves(value)
    stacked = jnp.concatenate(
        [jnp.concatenate([high, low], axis=1), jnp.concatenate([low, high], axis=1)], axis=0
    )
    both = lax.dot_general(
        stacked, packed, (((1,), (1,)), ((), ())), preferred_element_type=jnp.float32
    )
    return both[:rows] + both[rows:]


def times(value, packed):
    rows = value.shape[0]
    width = packed.shape[1] // 2
    high, low = halves(value)
    both = jnp.dot(
        jnp.concatenate([high, low], axis=0), packed, preferred_element_type=jnp.float32
    )
    summed = both[:rows] + both[rows:]
    return summed[:, :width] + summed[:, width:]


def kernel(
    levels, supers, rhs_hbm, inverse_hbm, factor_hbm, pattern_hbm, forward_ref, answer_ref,
    rhs, inverse, factor, pattern, inverse_packed, packed, terms, outbox, inbox, solved,
    load_sem, outbox_sem, inbox_sem, solved_sem, arrived_sem, *arrived,
):
    place = lax.axis_index("chain")
    me = lax.axis_index("col")
    count, _, width = factor.shape
    loads = rhs.shape[0]
    rows = loads // PIECES
    loading = [
        pltpu.make_async_copy(source, target, load_sem.at[at])
        for at, (source, target) in enumerate(
            ((rhs_hbm, rhs), (inverse_hbm, inverse), (factor_hbm, factor), (pattern_hbm, pattern))
        )
    ]
    for copy in loading:
        copy.start()
    peers = [lax.rem(me + shift, supers) for shift in range(supers)]

    barrier = pltpu.get_barrier_semaphore()

    @pl.when(place > 0)
    def _():
        for peer in peers:
            pl.semaphore_signal(
                barrier, inc=1, device_id={"chain": place - 1, "col": peer}, device_id_type=MESH
            )

    @pl.when(place < levels - 1)
    def _():
        for peer in peers:
            pl.semaphore_signal(
                barrier, inc=1, device_id={"chain": place + 1, "col": peer}, device_id_type=MESH
            )

    loading[0].wait()
    loading[1].wait()
    high, low = halves(inverse[...])
    inverse_packed[:, :width] = high
    inverse_packed[:, width:] = low

    def pack(block, value):
        high, low = halves(value)
        packed[block * width:(block + 1) * width, :width] = high
        packed[block * width:(block + 1) * width, width:] = low

    def pack_products():
        for block in range(count):
            pack(block, times(factor[block], inverse_packed[...]))

    loading[2].wait()
    loading[3].wait()
    targets = [pattern[0, 0, block] for block in range(count)]
    origin = []
    for peer in peers:
        at = jnp.int32(-1)
        for block in range(count):
            at = jnp.where(targets[block] == peer, jnp.int32(block), at)
        origin.append(at)
    slots = [lax.rem(me - target + supers, supers) for target in targets]

    @pl.when(place == 0)
    def _():
        for block in range(count):
            pack(block, factor[block])
        rhs[...] = times_transposed(rhs[...], inverse_packed[...])
        forward_ref[...] = rhs[...]

    @pl.when((place > 0) & (place < levels - 1))
    def _():
        pack_products()

    @pl.when(place == levels - 1)
    def _():
        pack(0, times(inverse[...].T, inverse_packed[...]))

    def term_copy(piece, shift):
        return pltpu.make_async_remote_copy(
            src_ref=outbox.at[piece, shift],
            dst_ref=inbox.at[piece, shift],
            send_sem=outbox_sem.at[piece, shift],
            recv_sem=inbox_sem.at[piece, shift],
            device_id={"chain": place + 1, "col": peers[shift]},
            device_id_type=MESH,
        )

    def answer_copy(piece, shift):
        return pltpu.make_async_remote_copy(
            src_ref=solved.at[piece],
            dst_ref=arrived[piece].at[shift],
            send_sem=solved_sem.at[piece, shift],
            recv_sem=arrived_sem.at[piece, shift],
            device_id={"chain": place - 1, "col": peers[shift]},
            device_id_type=MESH,
        )

    for piece in range(PIECES):
        part = pl.ds(piece * rows, rows)

        @pl.when(place > 0)
        def _():
            total = rhs[part, :]
            for shift in range(supers):
                pltpu.make_async_copy(
                    inbox.at[piece, shift], inbox.at[piece, shift], inbox_sem.at[piece, shift]
                ).wait()
                total = total - inbox[piece, shift]
            rhs[part, :] = total

        @pl.when(place < levels - 1)
        def _():
            wide = times_transposed(rhs[part, :], packed[...])
            for block in range(count):
                terms[block] = wide[:, block * width:(block + 1) * width]
            for shift in range(supers):
                picked = terms[jnp.maximum(origin[shift], 0)]
                if count < supers:
                    picked = jnp.where(origin[shift] >= 0, picked, 0.0)
                outbox[piece, shift] = picked

        @pl.when(place == levels - 1)
        def _():
            fresh = times(rhs[part, :], packed[:width, :])
            solved[piece] = fresh
            answer_ref[part, :] = fresh

        if piece == 0:
            pl.semaphore_wait(
                barrier, jnp.where(place > 0, supers, 0) + jnp.where(place < levels - 1, supers, 0)
            )

        @pl.when(place < levels - 1)
        def _():
            for shift in range(supers):
                term_copy(piece, shift).start()

        @pl.when(place == levels - 1)
        def _():
            for shift in range(supers):
                answer_copy(piece, shift).start()

    @pl.when(place > 0)
    def _():
        forward_ref[...] = times_transposed(rhs[...], inverse_packed[...])

    @pl.when(place == 0)
    def _():
        pack_products()

    @pl.when(place < levels - 1)
    def _():
        rhs[...] = times(forward_ref[...], inverse_packed[...])
        for piece in range(PIECES):
            part = pl.ds(piece * rows, rows)
            for shift in range(supers):
                pltpu.make_async_copy(
                    arrived[piece].at[shift], arrived[piece].at[shift], arrived_sem.at[piece, shift]
                ).wait()
            picked = jnp.concatenate([arrived[piece][slot] for slot in slots], axis=1)
            fresh = rhs[part, :] - times(picked, packed[...])
            solved[piece] = fresh
            answer_ref[part, :] = fresh

            @pl.when(place > 0)
            def _():
                for shift in range(supers):
                    answer_copy(piece, shift).start()

    @pl.when(place < levels - 1)
    def _():
        for piece in range(PIECES):
            for shift in range(supers):
                term_copy(piece, shift).wait_send()

    @pl.when(place > 0)
    def _():
        for piece in range(PIECES):
            for shift in range(supers):
                answer_copy(piece, shift).wait_send()


def body(rhs, inverse, factor, pattern):
    levels = lax.axis_size("chain")
    supers = lax.axis_size("col")
    loads, width = rhs.shape[2:]
    count = factor.shape[2]
    rows = loads // PIECES
    block = pltpu.VMEM((loads, width), jnp.float32)
    anywhere = pl.BlockSpec(memory_space=pl.ANY)
    solved, answer = pl.pallas_call(
        functools.partial(kernel, levels, supers),
        out_shape=(block, block),
        in_specs=[anywhere] * 4,
        out_specs=[pl.BlockSpec(memory_space=pltpu.VMEM)] * 2,
        scratch_shapes=[
            pltpu.VMEM((loads, width), jnp.float32),
            pltpu.VMEM((width, width), jnp.float32),
            pltpu.VMEM((count, width, width), jnp.float32),
            pltpu.SMEM((1, 1, count), jnp.int32),
            pltpu.VMEM((width, 2 * width), jnp.bfloat16),
            pltpu.VMEM((count * width, 2 * width), jnp.bfloat16),
            pltpu.VMEM((count, rows, width), jnp.float32),
            pltpu.VMEM((PIECES, supers, rows, width), jnp.float32),
            pltpu.VMEM((PIECES, supers, rows, width), jnp.float32),
            pltpu.VMEM((PIECES, rows, width), jnp.float32),
            pltpu.SemaphoreType.DMA((4,)),
            pltpu.SemaphoreType.DMA((PIECES, supers)),
            pltpu.SemaphoreType.DMA((PIECES, supers)),
            pltpu.SemaphoreType.DMA((PIECES, supers)),
            pltpu.SemaphoreType.DMA((PIECES, supers)),
            *[pltpu.VMEM((supers, rows, width), jnp.float32)] * PIECES,
        ],
        compiler_params=pltpu.CompilerParams(collective_id=0, has_side_effects=True),
    )(rhs[0, 0], inverse[0, 0], factor[0, 0], pattern)
    return (solved[None, None], answer[None, None])


def solution(mesh):
    in_specs = (
        P("chain", "col", None, None),
        P("chain", "col", None, None),
        P("chain", "col", None, None, None),
        P("chain", "col", None),
    )
    out_specs = (P("chain", "col", None, None), P("chain", "col", None, None))
    return jax.shard_map(body, mesh=mesh, in_specs=in_specs, out_specs=out_specs, check_vma=False)
```

```python
import functools

import jax
import jax.numpy as jnp
from jax import lax
from jax.experimental import pallas as pl
from jax.experimental.pallas import tpu as pltpu
from jax.sharding import PartitionSpec as P

PIECES = 4
MESH = pl.DeviceIdType.MESH


def halves(value):
    high = value.astype(jnp.bfloat16)
    low = (value - high.astype(jnp.float32)).astype(jnp.bfloat16)
    return high, low


def times_transposed(value, packed):
    rows = value.shape[0]
    high, low = halves(value)
    stacked = jnp.concatenate(
        [jnp.concatenate([high, low], axis=1), jnp.concatenate([low, high], axis=1)], axis=0
    )
    both = lax.dot_general(
        stacked, packed, (((1,), (1,)), ((), ())), preferred_element_type=jnp.float32
    )
    return both[:rows] + both[rows:]


def times_turned(value, turned):
    rows = value.shape[0]
    high, low = halves(value)
    stacked = jnp.concatenate(
        [jnp.concatenate([high, low], axis=1), jnp.concatenate([low, high], axis=1)], axis=0
    )
    both = jnp.dot(stacked, turned, preferred_element_type=jnp.float32)
    return both[:rows] + both[rows:]


def times(value, packed):
    rows = value.shape[0]
    width = packed.shape[1] // 2
    high, low = halves(value)
    both = jnp.dot(
        jnp.concatenate([high, low], axis=0), packed, preferred_element_type=jnp.float32
    )
    summed = both[:rows] + both[rows:]
    return summed[:, :width] + summed[:, width:]


def kernel(
    levels, supers, rhs_hbm, inverse_hbm, factor_hbm, pattern_hbm, both_ref,
    rhs, inverse, factor, pattern, inverse_packed, packed, turned, terms, outbox, inbox, solved,
    load_sem, outbox_sem, inbox_sem, solved_sem, arrived_sem, *arrived,
):
    forward_ref, answer_ref = both_ref.at[0], both_ref.at[1]
    place = lax.axis_index("chain")
    me = lax.axis_index("col")
    count, _, width = factor.shape
    loads = rhs.shape[0]
    rows = loads // PIECES
    loading = [
        pltpu.make_async_copy(source, target, load_sem.at[at])
        for at, (source, target) in enumerate(
            ((rhs_hbm, rhs), (inverse_hbm, inverse), (factor_hbm, factor), (pattern_hbm, pattern))
        )
    ]
    for copy in loading:
        copy.start()
    peers = [lax.rem(me + shift, supers) for shift in range(supers)]

    barrier = pltpu.get_barrier_semaphore()

    @pl.when(place > 0)
    def _():
        for peer in peers:
            pl.semaphore_signal(
                barrier, inc=1, device_id={"chain": place - 1, "col": peer}, device_id_type=MESH
            )

    @pl.when(place < levels - 1)
    def _():
        for peer in peers:
            pl.semaphore_signal(
                barrier, inc=1, device_id={"chain": place + 1, "col": peer}, device_id_type=MESH
            )

    loading[0].wait()
    loading[1].wait()
    high, low = halves(inverse[...])
    inverse_packed[:, :width] = high
    inverse_packed[:, width:] = low

    full = count == supers

    def pack(block, value):
        high, low = halves(value)
        packed[block * width:(block + 1) * width, :width] = high
        packed[block * width:(block + 1) * width, width:] = low

    def pack_turned(block, value):
        high, low = halves(value.T)
        turned[:width, block * width:(block + 1) * width] = high
        turned[width:, block * width:(block + 1) * width] = low

    def block_of(block):
        return factor[jnp.maximum(origin[block], 0)] if full else factor[block]

    loading[2].wait()
    loading[3].wait()
    targets = [pattern[0, 0, block] for block in range(count)]
    origin = []
    for peer in peers:
        at = jnp.int32(-1)
        for block in range(count):
            at = jnp.where(targets[block] == peer, jnp.int32(block), at)
        origin.append(at)
    slots = [lax.rem(me - target + supers, supers) for target in targets]

    @pl.when(place == 0)
    def _():
        for block in range(count):
            pack_turned(block, block_of(block))
        rhs[...] = times_transposed(rhs[...], inverse_packed[...])
        forward_ref[...] = rhs[...]

    @pl.when((place > 0) & (place < levels - 1))
    def _():
        for block in range(count):
            product = times(block_of(block), inverse_packed[...])
            pack(block, product)
            pack_turned(block, product)

    @pl.when(place == levels - 1)
    def _():
        pack(0, times(inverse[...].T, inverse_packed[...]))

    def term_copy(piece, shift):
        return pltpu.make_async_remote_copy(
            src_ref=outbox.at[piece, shift],
            dst_ref=inbox.at[piece, shift],
            send_sem=outbox_sem.at[piece, shift],
            recv_sem=inbox_sem.at[piece, shift],
            device_id={"chain": place + 1, "col": peers[shift]},
            device_id_type=MESH,
        )

    def answer_copy(piece, shift):
        return pltpu.make_async_remote_copy(
            src_ref=solved.at[piece],
            dst_ref=arrived[piece].at[shift],
            send_sem=solved_sem.at[piece, shift],
            recv_sem=arrived_sem.at[piece, shift],
            device_id={"chain": place - 1, "col": peers[shift]},
            device_id_type=MESH,
        )

    for piece in range(PIECES):
        part = pl.ds(piece * rows, rows)

        @pl.when(place > 0)
        def _():
            total = rhs[part, :]
            for shift in range(supers):
                pltpu.make_async_copy(
                    inbox.at[piece, shift], inbox.at[piece, shift], inbox_sem.at[piece, shift]
                ).wait()
                total = total - inbox[piece, shift]
            rhs[part, :] = total

        @pl.when(place < levels - 1)
        def _():
            wide = times_turned(rhs[part, :], turned[...])
            if full:
                for shift in range(supers):
                    outbox[piece, shift] = wide[:, shift * width:(shift + 1) * width]
            else:
                for block in range(count):
                    terms[block] = wide[:, block * width:(block + 1) * width]
                for shift in range(supers):
                    picked = terms[jnp.maximum(origin[shift], 0)]
                    outbox[piece, shift] = jnp.where(origin[shift] >= 0, picked, 0.0)

        @pl.when(place == levels - 1)
        def _():
            fresh = times(rhs[part, :], packed[:width, :])
            solved[piece] = fresh
            answer_ref[part, :] = fresh

        if piece == 0:
            pl.semaphore_wait(
                barrier, jnp.where(place > 0, supers, 0) + jnp.where(place < levels - 1, supers, 0)
            )

        @pl.when(place < levels - 1)
        def _():
            for shift in range(supers):
                term_copy(piece, shift).start()

        @pl.when(place == levels - 1)
        def _():
            for shift in range(supers):
                answer_copy(piece, shift).start()

    @pl.when(place > 0)
    def _():
        forward_ref[...] = times_transposed(rhs[...], inverse_packed[...])

    @pl.when(place == 0)
    def _():
        for block in range(count):
            pack(block, times(block_of(block), inverse_packed[...]))

    @pl.when(place < levels - 1)
    def _():
        rhs[...] = times(forward_ref[...], inverse_packed[...])
        for piece in range(PIECES):
            part = pl.ds(piece * rows, rows)
            for shift in range(supers):
                pltpu.make_async_copy(
                    arrived[piece].at[shift], arrived[piece].at[shift], arrived_sem.at[piece, shift]
                ).wait()
            if full:
                chosen = [arrived[piece][(supers - shift) % supers] for shift in range(supers)]
            else:
                chosen = [arrived[piece][slot] for slot in slots]
            picked = jnp.concatenate(chosen, axis=1)
            fresh = rhs[part, :] - times(picked, packed[...])
            solved[piece] = fresh
            answer_ref[part, :] = fresh

            @pl.when(place > 0)
            def _():
                for shift in range(supers):
                    answer_copy(piece, shift).start()

    @pl.when(place < levels - 1)
    def _():
        for piece in range(PIECES):
            for shift in range(supers):
                term_copy(piece, shift).wait_send()

    @pl.when(place > 0)
    def _():
        for piece in range(PIECES):
            for shift in range(supers):
                answer_copy(piece, shift).wait_send()


def body(rhs, inverse, factor, pattern):
    levels = lax.axis_size("chain")
    supers = lax.axis_size("col")
    loads, width = rhs.shape[2:]
    count = factor.shape[2]
    rows = loads // PIECES
    block = pltpu.VMEM((2, loads, width), jnp.float32)
    anywhere = pl.BlockSpec(memory_space=pl.ANY)
    both = pl.pallas_call(
        functools.partial(kernel, levels, supers),
        out_shape=block,
        in_specs=[anywhere] * 4,
        out_specs=pl.BlockSpec(memory_space=pltpu.VMEM),
        scratch_shapes=[
            pltpu.VMEM((loads, width), jnp.float32),
            pltpu.VMEM((width, width), jnp.float32),
            pltpu.VMEM((count, width, width), jnp.float32),
            pltpu.SMEM((1, 1, count), jnp.int32),
            pltpu.VMEM((width, 2 * width), jnp.bfloat16),
            pltpu.VMEM((count * width, 2 * width), jnp.bfloat16),
            pltpu.VMEM((2 * width, count * width), jnp.bfloat16),
            pltpu.VMEM((count, rows, width), jnp.float32),
            pltpu.VMEM((PIECES, supers, rows, width), jnp.float32),
            pltpu.VMEM((PIECES, supers, rows, width), jnp.float32),
            pltpu.VMEM((PIECES, rows, width), jnp.float32),
            pltpu.SemaphoreType.DMA((4,)),
            pltpu.SemaphoreType.DMA((PIECES, supers)),
            pltpu.SemaphoreType.DMA((PIECES, supers)),
            pltpu.SemaphoreType.DMA((PIECES, supers)),
            pltpu.SemaphoreType.DMA((PIECES, supers)),
            *[pltpu.VMEM((supers, rows, width), jnp.float32)] * PIECES,
        ],
        compiler_params=pltpu.CompilerParams(collective_id=0, has_side_effects=True),
    )(rhs[0, 0], inverse[0, 0], factor[0, 0], pattern)
    return (both[None, :1], both[None, 1:])


def solution(mesh):
    in_specs = (
        P("chain", "col", None, None),
        P("chain", "col", None, None),
        P("chain", "col", None, None, None),
        P("chain", "col", None),
    )
    out_specs = (P("chain", "col", None, None), P("chain", "col", None, None))
    return jax.shard_map(body, mesh=mesh, in_specs=in_specs, out_specs=out_specs, check_vma=False)
```

```python
import functools

import jax
import jax.numpy as jnp
from jax import lax
from jax.experimental import pallas as pl
from jax.experimental.pallas import tpu as pltpu
from jax.sharding import PartitionSpec as P

PIECES = 4
MESH = pl.DeviceIdType.MESH


def halves(value):
    high = value.astype(jnp.bfloat16)
    low = (value - high.astype(jnp.float32)).astype(jnp.bfloat16)
    return high, low


def times_transposed(value, packed):
    rows = value.shape[0]
    high, low = halves(value)
    stacked = jnp.concatenate(
        [jnp.concatenate([high, low], axis=1), jnp.concatenate([low, high], axis=1)], axis=0
    )
    both = lax.dot_general(
        stacked, packed, (((1,), (1,)), ((), ())), preferred_element_type=jnp.float32
    )
    return both[:rows] + both[rows:]


def times_turned(value, turned):
    rows = value.shape[0]
    high, low = halves(value)
    stacked = jnp.concatenate(
        [jnp.concatenate([high, low], axis=1), jnp.concatenate([low, high], axis=1)], axis=0
    )
    both = jnp.dot(stacked, turned, preferred_element_type=jnp.float32)
    return both[:rows] + both[rows:]


def times(value, packed):
    rows = value.shape[0]
    width = packed.shape[1] // 2
    high, low = halves(value)
    both = jnp.dot(
        jnp.concatenate([high, low], axis=0), packed, preferred_element_type=jnp.float32
    )
    summed = both[:rows] + both[rows:]
    return summed[:, :width] + summed[:, width:]


def kernel(
    levels, supers, rhs_hbm, inverse_hbm, factor_hbm, pattern_hbm, both_ref,
    rhs, inverse, factor, pattern, inverse_packed, packed, turned, terms, outbox, inbox, solved,
    load_sem, outbox_sem, inbox_sem, solved_sem, arrived_sem, *arrived,
):
    forward_ref, answer_ref = both_ref.at[0], both_ref.at[1]
    place = lax.axis_index("chain")
    me = lax.axis_index("col")
    count, _, width = factor.shape
    loads = rhs.shape[0]
    rows = loads // PIECES
    loading = [
        pltpu.make_async_copy(source, target, load_sem.at[at])
        for at, (source, target) in enumerate(
            ((rhs_hbm, rhs), (inverse_hbm, inverse), (factor_hbm, factor), (pattern_hbm, pattern))
        )
    ]
    for copy in loading:
        copy.start()
    peers = [lax.rem(me + shift, supers) for shift in range(supers)]

    barrier = pltpu.get_barrier_semaphore()

    @pl.when(place > 0)
    def _():
        for peer in peers:
            pl.semaphore_signal(
                barrier, inc=1, device_id={"chain": place - 1, "col": peer}, device_id_type=MESH
            )

    @pl.when(place < levels - 1)
    def _():
        for peer in peers:
            pl.semaphore_signal(
                barrier, inc=1, device_id={"chain": place + 1, "col": peer}, device_id_type=MESH
            )

    loading[0].wait()
    loading[1].wait()
    high, low = halves(inverse[...])
    inverse_packed[:, :width] = high
    inverse_packed[:, width:] = low

    full = count == supers

    def pack(block, value):
        high, low = halves(value)
        packed[block * width:(block + 1) * width, :width] = high
        packed[block * width:(block + 1) * width, width:] = low

    def pack_turned(block, value):
        high, low = halves(value.T)
        turned[:width, block * width:(block + 1) * width] = high
        turned[width:, block * width:(block + 1) * width] = low

    def block_of(block):
        return factor[jnp.maximum(origin[block], 0)] if full else factor[block]

    loading[2].wait()
    loading[3].wait()
    targets = [pattern[0, 0, block] for block in range(count)]
    origin = []
    for peer in peers:
        at = jnp.int32(-1)
        for block in range(count):
            at = jnp.where(targets[block] == peer, jnp.int32(block), at)
        origin.append(at)
    slots = [lax.rem(me - target + supers, supers) for target in targets]

    @pl.when(place == 0)
    def _():
        for block in range(count):
            pack_turned(block, block_of(block))
        rhs[...] = times_transposed(rhs[...], inverse_packed[...])
        forward_ref[...] = rhs[...]

    @pl.when((place > 0) & (place < levels - 1))
    def _():
        for block in range(count):
            product = times(block_of(block), inverse_packed[...])
            pack(block, product)
            pack_turned(block, product)

    @pl.when(place == levels - 1)
    def _():
        pack(0, times(inverse[...].T, inverse_packed[...]))

    def term_copy(piece, shift):
        return pltpu.make_async_remote_copy(
            src_ref=outbox.at[piece, shift],
            dst_ref=inbox.at[piece, shift],
            send_sem=outbox_sem.at[piece, shift],
            recv_sem=inbox_sem.at[piece],
            device_id={"chain": place + 1, "col": peers[shift]},
            device_id_type=MESH,
        )

    def answer_copy(piece, shift):
        return pltpu.make_async_remote_copy(
            src_ref=solved.at[piece],
            dst_ref=arrived[piece].at[shift],
            send_sem=solved_sem.at[piece, shift],
            recv_sem=arrived_sem.at[piece],
            device_id={"chain": place - 1, "col": peers[shift]},
            device_id_type=MESH,
        )

    for piece in range(PIECES):
        part = pl.ds(piece * rows, rows)

        @pl.when(place > 0)
        def _():
            pltpu.make_async_copy(inbox.at[piece], inbox.at[piece], inbox_sem.at[piece]).wait()
            total = rhs[part, :] - jnp.sum(inbox[piece], axis=0)
            rhs[part, :] = total

        @pl.when(place < levels - 1)
        def _():
            wide = times_turned(rhs[part, :], turned[...])
            if full:
                for shift in range(supers):
                    outbox[piece, shift] = wide[:, shift * width:(shift + 1) * width]
            else:
                for block in range(count):
                    terms[block] = wide[:, block * width:(block + 1) * width]
                for shift in range(supers):
                    picked = terms[jnp.maximum(origin[shift], 0)]
                    outbox[piece, shift] = jnp.where(origin[shift] >= 0, picked, 0.0)

        @pl.when(place == levels - 1)
        def _():
            fresh = times(rhs[part, :], packed[:width, :])
            solved[piece] = fresh
            answer_ref[part, :] = fresh

        if piece == 0:
            pl.semaphore_wait(
                barrier, jnp.where(place > 0, supers, 0) + jnp.where(place < levels - 1, supers, 0)
            )

        @pl.when(place < levels - 1)
        def _():
            for shift in range(supers):
                term_copy(piece, shift).start()

        @pl.when(place == levels - 1)
        def _():
            for shift in range(supers):
                answer_copy(piece, shift).start()

    @pl.when(place > 0)
    def _():
        forward_ref[...] = times_transposed(rhs[...], inverse_packed[...])

    @pl.when(place == 0)
    def _():
        for block in range(count):
            pack(block, times(block_of(block), inverse_packed[...]))

    @pl.when(place < levels - 1)
    def _():
        rhs[...] = times(forward_ref[...], inverse_packed[...])
        for piece in range(PIECES):
            part = pl.ds(piece * rows, rows)
            pltpu.make_async_copy(arrived[piece], arrived[piece], arrived_sem.at[piece]).wait()
            if full:
                chosen = [arrived[piece][(supers - shift) % supers] for shift in range(supers)]
            else:
                chosen = [arrived[piece][slot] for slot in slots]
            picked = jnp.concatenate(chosen, axis=1)
            fresh = rhs[part, :] - times(picked, packed[...])
            solved[piece] = fresh
            answer_ref[part, :] = fresh

            @pl.when(place > 0)
            def _():
                for shift in range(supers):
                    answer_copy(piece, shift).start()

    @pl.when(place < levels - 1)
    def _():
        for piece in range(PIECES):
            for shift in range(supers):
                term_copy(piece, shift).wait_send()

    @pl.when(place > 0)
    def _():
        for piece in range(PIECES):
            for shift in range(supers):
                answer_copy(piece, shift).wait_send()


def body(rhs, inverse, factor, pattern):
    levels = lax.axis_size("chain")
    supers = lax.axis_size("col")
    loads, width = rhs.shape[2:]
    count = factor.shape[2]
    rows = loads // PIECES
    block = pltpu.VMEM((2, loads, width), jnp.float32)
    anywhere = pl.BlockSpec(memory_space=pl.ANY)
    both = pl.pallas_call(
        functools.partial(kernel, levels, supers),
        out_shape=block,
        in_specs=[anywhere] * 4,
        out_specs=pl.BlockSpec(memory_space=pltpu.VMEM),
        scratch_shapes=[
            pltpu.VMEM((loads, width), jnp.float32),
            pltpu.VMEM((width, width), jnp.float32),
            pltpu.VMEM((count, width, width), jnp.float32),
            pltpu.SMEM((1, 1, count), jnp.int32),
            pltpu.VMEM((width, 2 * width), jnp.bfloat16),
            pltpu.VMEM((count * width, 2 * width), jnp.bfloat16),
            pltpu.VMEM((2 * width, count * width), jnp.bfloat16),
            pltpu.VMEM((count, rows, width), jnp.float32),
            pltpu.VMEM((PIECES, supers, rows, width), jnp.float32),
            pltpu.VMEM((PIECES, supers, rows, width), jnp.float32),
            pltpu.VMEM((PIECES, rows, width), jnp.float32),
            pltpu.SemaphoreType.DMA((4,)),
            pltpu.SemaphoreType.DMA((PIECES, supers)),
            pltpu.SemaphoreType.DMA((PIECES,)),
            pltpu.SemaphoreType.DMA((PIECES, supers)),
            pltpu.SemaphoreType.DMA((PIECES,)),
            *[pltpu.VMEM((supers, rows, width), jnp.float32)] * PIECES,
        ],
        compiler_params=pltpu.CompilerParams(collective_id=0, has_side_effects=True),
    )(rhs[0, 0], inverse[0, 0], factor[0, 0], pattern)
    return (both[None, :1], both[None, 1:])


def solution(mesh):
    in_specs = (
        P("chain", "col", None, None),
        P("chain", "col", None, None),
        P("chain", "col", None, None, None),
        P("chain", "col", None),
    )
    out_specs = (P("chain", "col", None, None), P("chain", "col", None, None))
    return jax.shard_map(body, mesh=mesh, in_specs=in_specs, out_specs=out_specs, check_vma=False)
```
